32 devices in a mesh: row: 8 (over y, x, core), col: 4 (over z).
Axes of the slice: x: 2, y: 2, z: 4, core: 2. Of those that a mesh axis runs over, the one named last changes fastest.
Arguments:
- spectra: float32 [2, 3, 8, 512, 1024], P(None, None, 'row', 'col'), may hold values from -6 to 6
- history: bfloat16 [16, 3, 8, 128, 128], P(None, None, 'row', 'col'), as said below
- steps: int32 [16], replicated, may hold values from 0 to 15, each once
- basis: bfloat16 [256, 3, 8, 128, 128], P(None, None, 'row', 'col'), as said below
Outputs:
- velocity: float32 [3, 8, 1024, 1024], P(None, 'row', 'col')
- coeffs: float32 [256, 16], replicated
- factor: float32 [16, 16], replicated
- ortho: float32 [16, 3, 8, 128, 128], P(None, None, 'row', 'col')
The draws below stay inside these ranges and needn't reach their ends.
Inputs may be any that keep to these rules, and one draw needn't show every extreme that they name: `steps`: each stored snapshot index appears once. `history`: every entry lies between -0.75 and 0.75. `basis`: every entry is at most 6 / sqrt(393216) in magnitude.
All inputs are finite; a program needn't handle non-finite values.
Results may differ from the reference program's by a relative error of at most 0.0012.
Values sent between devices are 32-bit elements; how exact they have to be, the bound alone decides.
No kernel may reach another device: no remote copies, remote signals or barrier semaphores. Data moves between devices by JAX's collectives and lax.ppermute only.
A program may use at most 128 MiB of HBM per device.

```python
import math
import jax
import jax.numpy as jnp
from jax import lax

GRID = 1024
MODES = 512
STRIDE = 8
RANK = 256
SNAPS = 16
HIST = 16
NZ = 8
CELLS = 128
ROWS = 393216


def shared_rows(key):
    basis_key = jax.random.fold_in(key, 7101)
    raw = jax.random.normal(basis_key, (RANK, ROWS), jnp.float32)
    return jnp.clip(raw, -6.0, 6.0) / math.sqrt(ROWS)


def draw_basis(key, part):
    basis_rows = shared_rows(key)
    return basis_rows.reshape(RANK, 3, NZ, CELLS, CELLS).astype(jnp.bfloat16)


def draw_history(key, part):
    basis_rows = shared_rows(key)
    exponent = jax.random.uniform(jax.random.fold_in(key, 7201), (RANK,), jnp.float32, 0.0, 1.0)
    decay = jnp.exp(-exponent * math.log(10.0))
    own_part = jax.random.normal(jax.random.fold_in(key, 7202), (HIST, RANK), jnp.float32)
    mixture = own_part
    noise = jax.random.normal(jax.random.fold_in(key, 7204), (HIST, ROWS), jnp.float32)
    share = jax.random.uniform(jax.random.fold_in(key, 7205), (HIST, 1), jnp.float32, 0.25, 0.45)
    scaling = 0.125 * jnp.ones((HIST, 1), jnp.float32)
    weights = mixture * decay[None, :]
    weights = weights / jnp.sqrt(jnp.sum(weights * weights, axis=1, keepdims=True))
    inside = jnp.dot(weights, basis_rows, precision=lax.Precision.HIGHEST)
    outside = noise / math.sqrt(ROWS)
    flat = scaling * math.sqrt(ROWS) * (jnp.sqrt(1.0 - share * share) * inside + share * outside)
    flat = jnp.clip(flat, -0.75, 0.75)
    return flat.reshape(HIST, 3, NZ, CELLS, CELLS).astype(jnp.bfloat16)


def levels(own_key, extent, shards, least, largest):
    def one(axis_at, blocks):
        steps = jax.random.uniform(jax.random.fold_in(jax.random.fold_in(own_key, 6), axis_at), (blocks,), jnp.float32, least / len(shards), largest / len(shards))
        return jnp.repeat(jnp.exp(steps), extent[axis_at] // blocks).reshape((-1,) + (1,) * (len(extent) - axis_at - 1))

    loudness = one(*shards[0])
    for cut in shards[1:]:
        loudness = loudness * one(*cut)
    return loudness


def centred(rng, dims, width, most, split=(), held_as=jnp.bfloat16):
    entries = jax.random.normal(rng, dims, jnp.float32) * width
    if len(split) > 0:
        entries = levels(rng, dims, split, -0.22, 0.18) * entries
    return jnp.clip(entries, min=-most, max=most).astype(held_as)


def setup_inputs(seed: int = 0) -> dict:
    keys = jax.random.split(jax.random.key(seed), 5)
    spectra = centred(keys[0], (2, 3, NZ, MODES, GRID), 1.0, 6.0, ((2, 8), (3, 4)), jnp.float32)
    history = draw_history(jax.random.fold_in(keys[4], 71), 0)
    steps = jax.random.permutation(keys[2], HIST).astype(jnp.int32)
    basis = draw_basis(jax.random.fold_in(keys[4], 71), 0)
    return dict(spectra=spectra, history=history, steps=steps, basis=basis)


def tables(grid_len, mode_count):
    index_y = jnp.arange(grid_len, dtype=jnp.int32)
    phase_y = 2.0 * math.pi / grid_len * (index_y[:, None] * index_y[None, :] % grid_len).astype(jnp.float32)
    modes_x = jnp.arange(mode_count, dtype=jnp.int32)
    phase_x = 2.0 * math.pi / grid_len * (modes_x[:, None] * index_y[None, :] % grid_len).astype(jnp.float32)
    weight_x = jnp.where(modes_x == 0, 1.0, 2.0).astype(jnp.float32)[:, None] / grid_len
    table_x = jnp.stack([weight_x * jnp.cos(phase_x), -weight_x * jnp.sin(phase_x)])
    return (jnp.cos(phase_y), jnp.sin(phase_y), table_x)

def reference(spectra, history, steps, basis):
    highest = lax.Precision.HIGHEST
    cos_y, sin_y, table_x = tables(GRID, MODES)

    def plane_space(plane):
        wave_real = jnp.dot(plane[0], cos_y, precision=highest) - jnp.dot(plane[1], sin_y, precision=highest)
        wave_imag = jnp.dot(plane[0], sin_y, precision=highest) + jnp.dot(plane[1], cos_y, precision=highest)
        wave = jnp.stack([wave_real, wave_imag])
        return lax.dot_general(wave, table_x, (((0, 2), (0, 1)), ((), ())), precision=highest)
    planes = lax.map(plane_space, jnp.moveaxis(spectra, 2, 0))
    velocity = jnp.moveaxis(planes, 0, 1)
    coarse = velocity.reshape(3, NZ, CELLS, STRIDE, CELLS, STRIDE).mean(axis=(3, 5)).astype(jnp.bfloat16)
    chosen = jnp.take(history, steps[:SNAPS - 1], axis=0)
    snapshots = jnp.concatenate([coarse[None], chosen], axis=0)
    snap_flat = snapshots.reshape(SNAPS, ROWS)
    basis_flat = basis.reshape(RANK, ROWS)
    coeffs = lax.dot_general(basis_flat.astype(jnp.float32), snap_flat.astype(jnp.float32), (((1,), (1,)), ((), ())), preferred_element_type=jnp.float32)
    coeffs_high = coeffs.astype(jnp.bfloat16)
    coeffs_low = (coeffs - lax.optimization_barrier(coeffs_high).astype(jnp.float32)).astype(jnp.bfloat16)
    projected = lax.dot_general(coeffs_high.astype(jnp.float32), basis_flat.astype(jnp.float32), (((0,), (0,)), ((), ())), preferred_element_type=jnp.float32)
    projected = projected + lax.dot_general(coeffs_low.astype(jnp.float32), basis_flat.astype(jnp.float32), (((0,), (0,)), ((), ())), preferred_element_type=jnp.float32)
    residual = snap_flat.astype(jnp.float32) - projected
    gram_matrix = lax.dot_general(residual, residual, (((1,), (1,)), ((), ())), precision=highest) / ROWS
    lower_factor = jnp.linalg.cholesky(gram_matrix)
    ortho_flat = lax.linalg.triangular_solve(lower_factor, residual, left_side=True, lower=True)
    return (velocity, coeffs, lower_factor.T, ortho_flat.reshape(SNAPS, 3, NZ, CELLS, CELLS))
```

```python
import functools
import math

import jax
import jax.numpy as jnp
import ml_dtypes
import numpy as np
from jax import lax
from jax.experimental import pallas as pl
from jax.experimental.pallas import tpu as pltpu
from jax.sharding import PartitionSpec as P

STRIDE = 8
SNAPS = 16
RADIX = 4
LANES = 128
NT = (((1,), (1,)), ((), ()))


def halves(table):
    table = table.astype(np.float32)
    high = table.astype(ml_dtypes.bfloat16)
    low = (table - high.astype(np.float32)).astype(ml_dtypes.bfloat16)
    return np.stack([high, low])


@functools.lru_cache(maxsize=None)
def tables(grid_len, mode_count, col_count, stride):
    local = mode_count // col_count
    quarter = grid_len // RADIX
    index = np.arange(quarter)
    phase = 2.0 * np.pi / quarter * (index[:, None] * index[None, :] % quarter)
    dft = halves(np.concatenate([np.cos(phase), -np.sin(phase)], axis=1))
    twiddle_phase = 2.0 * np.pi / grid_len * np.arange(RADIX)[:, None] * index[None, :]
    twiddle = np.zeros((2 * RADIX, quarter), np.float32)
    twiddle[0::2] = np.cos(twiddle_phase)
    twiddle[1::2] = np.sin(twiddle_phase)
    modes = np.arange(mode_count)
    weight = np.where(modes == 0, 1.0, 2.0)[:, None] / grid_len
    place = np.arange(grid_len)
    phase = 2.0 * np.pi / grid_len * (modes[:, None] * place[None, :] % grid_len)
    full = np.stack([weight * np.cos(phase), -weight * np.sin(phase)])
    full = full.reshape(2, col_count, local // 2, 2, grid_len).transpose(1, 3, 0, 2, 4)
    along_x = halves(full.reshape(col_count, 2, local, grid_len)[..., : grid_len // 2])
    mean = full.reshape(col_count, 2 * local, grid_len // stride, stride).sum(-1) / stride**2
    return dft, twiddle, along_x, halves(mean)


def split(value):
    high = value.astype(jnp.bfloat16)
    return high, (value - high.astype(jnp.float32)).astype(jnp.bfloat16)


def product(left, right, dims):
    dot = functools.partial(
        lax.dot_general, dimension_numbers=dims, preferred_element_type=jnp.float32
    )
    return dot(left[0], right[0]) + (dot(left[0], right[1]) + dot(left[1], right[0]))


def wave_kernel(col_count, col_ref, spec_ref, dft_ref, twiddle_ref, mean_ref, *refs):
    out_refs, part_ref = refs[:col_count], refs[col_count]
    wave_ref, sum_ref, lane_ref = refs[col_count + 1 :]
    local, grid_len = spec_ref.shape[-2:]
    quarter = grid_len // RADIX
    block = quarter // col_count
    col = col_ref[0]
    dft = (dft_ref[0], dft_ref[1])
    for part in range(2):
        for lane in range(grid_len // LANES):
            lane_ref[part, lane] = spec_ref[part, 0, 0, :, lane * LANES : (lane + 1) * LANES]

    def piece(parity, part, r):
        per = quarter // LANES
        rows = pl.ds(parity, local // 2, stride=2)
        return jnp.concatenate(
            [lane_ref[part, lane, rows, :] for lane in range(r * per, (r + 1) * per)], axis=1
        )

    for t in range(RADIX):
        cosine, sine = twiddle_ref[2 * t : 2 * t + 1, :], twiddle_ref[2 * t + 1 : 2 * t + 2, :]
        first, second = [], []
        for parity in range(2):
            re = [piece(parity, 0, r) for r in range(RADIX)]
            im = [piece(parity, 1, r) for r in range(RADIX)]
            sign = 1.0 if t < 2 else -1.0
            if t % 2 == 0:
                u_re = (re[0] + re[2]) + sign * (re[1] + re[3])
                u_im = (im[0] + im[2]) + sign * (im[1] + im[3])
            else:
                u_re = (re[0] - re[2]) - sign * (im[1] - im[3])
                u_im = (im[0] - im[2]) + sign * (re[1] - re[3])
            if t == 0:
                v_re, v_im = u_re, u_im
            else:
                v_re = u_re * cosine - u_im * sine
                v_im = u_re * sine + u_im * cosine
            first += [v_re, v_im]
            second += [v_im, -v_re]
        rows = jnp.concatenate(
            [jnp.concatenate(first, axis=0), jnp.concatenate(second, axis=0)], axis=1
        )
        wave = product(dft, split(rows), NT)
        wave_ref[t] = wave
        for lane in range(2 * local // LANES):
            some = wave[:, lane * LANES : (lane + 1) * LANES]
            sum_ref[lane] = some if t == 0 else sum_ref[lane] + some
    for shift in range(col_count):
        start = pl.multiple_of(lax.rem(col + shift, col_count) * block, block)
        for t in range(RADIX):
            out_refs[shift][0, t * block : (t + 1) * block, :] = wave_ref[t, pl.ds(start, block), :]
    pair = STRIDE // RADIX
    total = []
    for lane in range(2 * local // LANES):
        steps = [sum_ref[lane, pl.ds(n, quarter // pair, stride=pair), :] for n in range(pair)]
        total.append(functools.reduce(jnp.add, steps))
    total = jnp.concatenate(total, axis=1)
    part_ref[0] = product(split(total), (mean_ref[0, 0], mean_ref[1, 0]), (((1,), (0,)), ((), ())))


def transform_y(col, spectra, consts, first, count, col_count):
    dft, twiddle, _, mean = consts
    local, grid_len = spectra.shape[-2:]
    quarter = grid_len // RADIX
    rows = grid_len // col_count
    cells = grid_len // STRIDE
    whole = lambda array: pl.BlockSpec(array.shape, lambda b, col: (0,) * array.ndim)
    out = jax.ShapeDtypeStruct((count, rows, 2 * local), jnp.float32)
    return pl.pallas_call(
        functools.partial(wave_kernel, col_count),
        grid_spec=pltpu.PrefetchScalarGridSpec(
            num_scalar_prefetch=1,
            grid=(count,),
            in_specs=[
                pl.BlockSpec((2, 1, 1, local, grid_len), lambda b, col: (0, first + b, 0, 0, 0)),
                whole(dft),
                whole(twiddle),
                pl.BlockSpec((2, 1, 2 * local, cells), lambda b, col: (0, col[0], 0, 0)),
            ],
            out_specs=[pl.BlockSpec((1, rows, 2 * local), lambda b, col: (b, 0, 0))] * col_count
            + [pl.BlockSpec((1, cells, cells), lambda b, col: (b, 0, 0))],
            scratch_shapes=[
                pltpu.VMEM((RADIX, quarter, 2 * local), jnp.float32),
                pltpu.VMEM((2 * local // LANES, quarter, LANES), jnp.float32),
                pltpu.VMEM((2, grid_len // LANES, local, LANES), jnp.float32),
            ],
        ),
        out_shape=[out] * col_count + [jax.ShapeDtypeStruct((count, cells, cells), jnp.float32)],
        name="transform_y",
    )(col, spectra, dft, twiddle, mean)


def field_kernel(col_count, col_ref, *refs):
    wave_refs, table_ref, out_ref, lane_ref = refs[:col_count], refs[col_count], refs[-2], refs[-1]
    rows, width = wave_refs[0].shape[-2:]
    local = width // 2
    block = rows // RADIX
    col = col_ref[0]
    sums = []
    for parity in range(2):
        lanes = slice(parity * local, (parity + 1) * local)
        wave = split(jnp.concatenate([ref[0, :, lanes] for ref in wave_refs], axis=1))
        table = []
        for half in range(2):
            table.append(
                jnp.concatenate(
                    [
                        table_ref[half, lax.rem(col + col_count - shift, col_count), parity]
                        for shift in range(col_count)
                    ],
                    axis=0,
                )
            )
        sums.append(product(wave, table, (((1,), (0,)), ((), ()))))
    half_len = out_ref.shape[-1] // 2
    for side, field in enumerate((sums[0] + sums[1], sums[0] - sums[1])):
        for lane in range(half_len // LANES):
            at = side * (half_len // LANES) + lane
            for t in range(RADIX):
                lane_ref[at, pl.ds(t, block, stride=RADIX), :] = field[
                    t * block : (t + 1) * block, lane * LANES : (lane + 1) * LANES
                ]
            out_ref[0, 0, :, at * LANES : (at + 1) * LANES] = lane_ref[at]


def transform_x(col, waves, at, table, velocity, component, shape, col_count):
    rows, width = waves[0].shape[-2:]
    in_specs = [
        pl.BlockSpec((1, rows, width), functools.partial(lambda b, i, col: (b, 0, 0), b))
        for b in at
    ] + [pl.BlockSpec(table.shape, lambda i, col: (0,) * table.ndim)]
    args = list(waves) + [table]
    aliases = {}
    if velocity is not None:
        in_specs.append(pl.BlockSpec(memory_space=pl.ANY))
        args.append(velocity)
        aliases = {len(args): 0}
    return pl.pallas_call(
        functools.partial(field_kernel, col_count),
        grid_spec=pltpu.PrefetchScalarGridSpec(
            num_scalar_prefetch=1,
            grid=(1,),
            in_specs=in_specs,
            out_specs=pl.BlockSpec((1, 1) + shape[2:], lambda i, col: (component, 0, 0, 0)),
            scratch_shapes=[pltpu.VMEM((shape[3] // LANES, rows, LANES), jnp.float32)],
        ),
        out_shape=jax.ShapeDtypeStruct(shape, jnp.float32),
        input_output_aliases=aliases,
        name="transform_x",
    )(col, *args)


def swap(value, axis, bit):
    size = lax.axis_size(axis)
    return lax.ppermute(value, axis, [(i, i ^ bit) for i in range(size)])


def sum_over(value, axis):
    bit, size = 1, lax.axis_size(axis)
    while bit < size:
        if 2 * bit < size:
            one, two, three = (swap(value, axis, bit * n) for n in (1, 2, 3))
            value = (value + one) + (two + three)
            bit *= 4
        else:
            value = value + swap(value, axis, bit)
            bit *= 2
    return value


def scatter_sum(value, axis, dim):
    size = lax.axis_size(axis)
    me = lax.axis_index(axis)
    shape = value.shape
    block = shape[dim] // size
    bits = size.bit_length() - 1
    value = value.reshape(shape[:dim] + (2,) * bits + (block,) + shape[dim + 1 :])
    for level in range(bits):
        at = dim + bits - 1 - level
        mine = (me >> level) & 1
        keep = lax.dynamic_index_in_dim(value, mine, at, keepdims=False)
        send = lax.dynamic_index_in_dim(value, 1 - mine, at, keepdims=False)
        value = keep + swap(send, axis, 1 << level)
    return value


def split_coeffs(coeffs):
    coeffs_high = coeffs.astype(jnp.bfloat16)
    high_wide = lax.optimization_barrier(coeffs_high).astype(jnp.float32)
    coeffs_low = (coeffs - high_wide).astype(jnp.bfloat16)
    return coeffs_high, lax.optimization_barrier(coeffs_low)


def update(coarse, history, steps, basis):
    chosen = jnp.take(history, steps[: SNAPS - 1], axis=0)
    snapshots = jnp.concatenate([coarse[None], chosen], axis=0)
    snap_flat = snapshots.reshape(SNAPS, -1)
    basis_flat = basis.reshape(basis.shape[0], -1)
    total_rows = snap_flat.shape[1] * lax.axis_size("row") * lax.axis_size("col")
    local_coeffs = lax.dot_general(basis_flat, snap_flat, NT, preferred_element_type=jnp.float32)
    coeffs = sum_over(sum_over(local_coeffs, "col"), "row")
    parts = jnp.concatenate(split_coeffs(coeffs), axis=1)
    projected = lax.dot_general(
        parts, basis_flat, (((0,), (0,)), ((), ())), preferred_element_type=jnp.float32
    )
    residual = snap_flat.astype(jnp.float32) - (projected[:SNAPS] + projected[SNAPS:])
    local_gram = lax.dot_general(residual, residual, NT, precision=lax.Precision.HIGHEST)
    gram = sum_over(sum_over(local_gram, "col"), "row") / total_rows
    lower_factor = jnp.linalg.cholesky(gram)
    ortho = lax.linalg.triangular_solve(lower_factor, residual, left_side=True, lower=True)
    return coeffs, lower_factor.T, ortho.reshape(snapshots.shape)


def body(spectra, history, steps, basis):
    grid_len = spectra.shape[4]
    components = spectra.shape[1]
    col_count = lax.axis_size("col")
    mode_count = spectra.shape[3] * col_count
    consts = [jnp.asarray(table) for table in tables(grid_len, mode_count, col_count, STRIDE)]
    col = lax.axis_index("col").astype(jnp.int32).reshape(1)
    groups = [(0, 1), (1, components - 1)]
    waves, parts = {}, []
    for first, count in groups:
        *out, part = transform_y(col, spectra, consts, first, count, col_count)
        parts.append(part)
        for b in range(count):
            moved = [(out[0], b)]
            for shift in range(1, col_count):
                perm = [(i, (i + shift) % col_count) for i in range(col_count)]
                moved.append((lax.ppermute(out[shift][b : b + 1], "col", perm), 0))
            waves[first + b] = moved
    part = jnp.concatenate(parts, axis=0)
    coarse = scatter_sum(part, "col", 1).astype(jnp.bfloat16)[:, None]
    coeffs, factor, ortho = update(coarse, history, steps, basis)
    shape = (components, 1, grid_len // col_count, grid_len)
    velocity = None
    for component in range(components):
        arrays, at = zip(*waves[component])
        velocity = transform_x(
            col, arrays, at, consts[2], velocity, component, shape, col_count
        )
    return velocity, coeffs, factor, ortho


def body_general(spectra, history, steps, basis):
    highest = lax.Precision.HIGHEST
    grid_len = spectra.shape[4]
    col_count = lax.axis_size("col")
    mode_count = spectra.shape[3] * col_count
    index_y = jnp.arange(grid_len, dtype=jnp.int32)
    phase_y = (
        2.0
        * math.pi
        / grid_len
        * (index_y[:, None] * index_y[None, :] % grid_len).astype(jnp.float32)
    )
    cos_y = jnp.cos(phase_y)
    sin_y = jnp.sin(phase_y)
    wave_real = jnp.dot(spectra[0], cos_y, precision=highest) - jnp.dot(
        spectra[1], sin_y, precision=highest
    )
    wave_imag = jnp.dot(spectra[0], sin_y, precision=highest) + jnp.dot(
        spectra[1], cos_y, precision=highest
    )
    wave = jnp.stack([wave_real, wave_imag])
    modes_x = jnp.arange(mode_count, dtype=jnp.int32)
    phase_x = (
        2.0
        * math.pi
        / grid_len
        * (modes_x[:, None] * index_y[None, :] % grid_len).astype(jnp.float32)
    )
    weight_x = jnp.where(modes_x == 0, 1.0, 2.0).astype(jnp.float32)[:, None] / grid_len
    table_x = jnp.stack([weight_x * jnp.cos(phase_x), -weight_x * jnp.sin(phase_x)])
    velocity = lax.dot_general(
        lax.all_to_all(wave, "col", split_axis=4, concat_axis=3, tiled=True),
        table_x,
        (((0, 3), (0, 1)), ((), ())),
        precision=highest,
    )
    components, planes, local_y, _ = velocity.shape
    coarse = (
        velocity.reshape(components, planes, local_y // STRIDE, STRIDE, grid_len // STRIDE, STRIDE)
        .mean(axis=(3, 5))
        .astype(jnp.bfloat16)
    )
    return (velocity,) + update(coarse, history, steps, basis)


def solution(mesh):
    in_specs = (
        P(None, None, "row", "col", None),
        P(None, None, "row", "col", None),
        P(),
        P(None, None, "row", "col", None),
    )
    out_specs = (P(None, "row", "col", None), P(), P(), P(None, None, "row", "col", None))

    def local_body(spectra, history, steps, basis):
        fits = spectra.shape[2] == 1 and spectra.shape[3] % 128 == 0
        return (body if fits else body_general)(spectra, history, steps, basis)

    return jax.shard_map(
        local_body, mesh=mesh, in_specs=in_specs, out_specs=out_specs, check_vma=False
    )
```

```python
import functools
import math

import jax
import jax.numpy as jnp
import ml_dtypes
import numpy as np
from jax import lax
from jax.experimental import pallas as pl
from jax.experimental.pallas import tpu as pltpu
from jax.sharding import PartitionSpec as P


STRIDE = 8
SNAPS = 16
RADIX = 4
LANES = 128
TAIL = 8
TILE = 16
NT = (((1,), (1,)), ((), ()))
NN = (((1,), (0,)), ((), ()))


def halves(table):
    table = table.astype(np.float32)
    high = table.astype(ml_dtypes.bfloat16)
    low = (table - high.astype(np.float32)).astype(ml_dtypes.bfloat16)
    return np.stack([high, low])


@functools.lru_cache(maxsize=None)
def tables(grid_len, mode_count, col_count, stride):
    local = mode_count // col_count
    quarter = grid_len // RADIX
    index = np.arange(quarter)
    phase = 2.0 * np.pi / quarter * (index[:, None] * index[None, :] % quarter)
    dft = halves(np.concatenate([np.cos(phase), -np.sin(phase)], axis=1))
    twiddle_phase = 2.0 * np.pi / grid_len * np.arange(RADIX)[:, None] * index[None, :]
    twiddle = np.zeros((2 * RADIX, quarter), np.float32)
    twiddle[0::2] = np.cos(twiddle_phase)
    twiddle[1::2] = np.sin(twiddle_phase)
    modes = np.arange(mode_count)
    weight = np.where(modes == 0, 1.0, 2.0)[:, None] / grid_len
    place = np.arange(grid_len)
    phase = 2.0 * np.pi / grid_len * (modes[:, None] * place[None, :] % grid_len)
    full = np.stack([weight * np.cos(phase), -weight * np.sin(phase)])
    full = full.reshape(2, col_count, local // 2, 2, grid_len).transpose(1, 3, 0, 2, 4)
    along_x = halves(full.reshape(col_count, 2, local, grid_len)[..., : grid_len // 2])
    mean = full.reshape(col_count, 2 * local, grid_len // stride, stride).sum(-1) / stride**2
    return dft, twiddle, along_x, halves(mean)


def in_hbm(array):
    return pltpu.with_memory_space_constraint(array, pltpu.HBM)


def in_vmem(array):
    return pltpu.with_memory_space_constraint(array, pltpu.VMEM)


def split(value):
    high = value.astype(jnp.bfloat16)
    return high, (value - high.astype(jnp.float32)).astype(jnp.bfloat16)


def product(left, right, dims):
    dot = functools.partial(
        lax.dot_general, dimension_numbers=dims, preferred_element_type=jnp.float32
    )
    return dot(left[0], right[0]) + (dot(left[0], right[1]) + dot(left[1], right[0]))


def wave_kernel(first, count, final, plan, col_ref, spec_hbm, dft_hbm, twiddle_hbm, mean_hbm, *refs):
    spec_ref, dft_ref, twiddle_ref, mean_ref, sum_ref, lane_ref, sems = refs[-7:]
    others, refs = refs[: first if final else 0], refs[first if final else 0 : -7]
    local, grid_len = spec_ref.shape[-2:]
    quarter = grid_len // RADIX
    col_count = 1 + max(shift for _, shift, _, _ in plan)
    out_refs, part_refs = refs[: len(plan)], refs[len(plan) :]
    block = quarter // col_count
    col = col_ref[0]
    copies = []
    for b in range(count):
        copies.append(
            pltpu.make_async_copy(spec_hbm.at[:, first + b, 0], spec_ref.at[b], sems.at[b])
        )
    copies.append(pltpu.make_async_copy(dft_hbm, dft_ref, sems.at[count]))
    copies.append(pltpu.make_async_copy(mean_hbm.at[:, col], mean_ref, sems.at[count + 1]))
    copies.append(pltpu.make_async_copy(twiddle_hbm, twiddle_ref, sems.at[count + 2]))
    for copy in copies:
        copy.start()
    starts = [
        pl.multiple_of(lax.rem(col + shift, col_count) * block, block) for shift in range(col_count)
    ]
    for b in range(count):
        copies[b].wait()
        for part in range(2):
            for lane in range(grid_len // LANES):
                lane_ref[part, lane] = spec_ref[b, part, :, lane * LANES : (lane + 1) * LANES]
        if b == 0:
            copies[count].wait()
            copies[count + 2].wait()
        dft = [
            jnp.concatenate([dft_ref[half, pl.ds(start, block), :] for start in starts], axis=0)
            for half in range(2)
        ]

        def piece(parity, part, r):
            per = quarter // LANES
            rows = pl.ds(parity, local // 2, stride=2)
            return jnp.concatenate(
                [lane_ref[part, lane, rows, :] for lane in range(r * per, (r + 1) * per)], axis=1
            )

        even_odd = {}
        for parity in range(2):
            for part in range(2):
                s0, s1, s2, s3 = [piece(parity, part, r) for r in range(RADIX)]
                even_odd[parity, part] = (s0 + s2, s1 + s3, s0 - s2, s1 - s3)
        for t in range(RADIX):
            cosine, sine = twiddle_ref[2 * t : 2 * t + 1, :], twiddle_ref[2 * t + 1 : 2 * t + 2, :]
            first_half, second_half = [], []
            for parity in range(2):
                re, im = even_odd[parity, 0], even_odd[parity, 1]
                if t == 0:
                    u_re, u_im = re[0] + re[1], im[0] + im[1]
                elif t == 2:
                    u_re, u_im = re[0] - re[1], im[0] - im[1]
                elif t == 1:
                    u_re, u_im = re[2] - im[3], im[2] + re[3]
                else:
                    u_re, u_im = re[2] + im[3], im[2] - re[3]
                if t == 0:
                    v_re, v_im = u_re, u_im
                else:
                    v_re = u_re * cosine - u_im * sine
                    v_im = u_re * sine + u_im * cosine
                first_half += [v_re, v_im]
                second_half += [v_im, -v_re]
            rows = jnp.concatenate(
                [jnp.concatenate(first_half, axis=0), jnp.concatenate(second_half, axis=0)], axis=1
            )
            wave = product(dft, split(rows), NT)
            for out_ref, (at, shift, n, size) in zip(out_refs, plan):
                if at == b:
                    start = shift * block + n * size
                    out_ref[t * size : (t + 1) * size, :] = wave[start : start + size]
            for lane in range(2 * local // LANES):
                some = wave[:, lane * LANES : (lane + 1) * LANES]
                sum_ref[lane] = some if t == 0 else sum_ref[lane] + some
        if b == 0:
            copies[count + 1].wait()
        pair = STRIDE // RADIX
        total = []
        for lane in range(2 * local // LANES):
            steps = [sum_ref[lane, pl.ds(n, quarter // pair, stride=pair), :] for n in range(pair)]
            total.append(functools.reduce(jnp.add, steps))
        total = jnp.concatenate(total, axis=1)
        mean = product(split(total), (mean_ref[0], mean_ref[1]), NN)
        if final:
            per = mean.shape[0] // col_count
            for shift in range(col_count):
                part_refs[shift][first + b] = mean[shift * per : (shift + 1) * per]
        else:
            part_refs[b][...] = mean
    for at, other in enumerate(others):
        per = other.shape[0] // col_count
        for shift in range(col_count):
            part_refs[shift][at] = other[shift * per : (shift + 1) * per]


def transform_y(col, spectra, consts, others, first, count, col_count, final):
    dft, twiddle, _, mean = consts
    components, (local, grid_len) = spectra.shape[1], spectra.shape[-2:]
    quarter = grid_len // RADIX
    rows = grid_len // col_count
    cells = grid_len // STRIDE
    vmem, hbm = pl.BlockSpec(memory_space=pltpu.VMEM), pl.BlockSpec(memory_space=pltpu.HBM)
    smem = pl.BlockSpec(memory_space=pltpu.SMEM)
    plan, outs = [], []
    for b in range(count):
        for shift in range(col_count):
            halves_of = 2 if final and b == count - 1 else 1
            for n in range(halves_of):
                plan.append((b, shift, n, rows // RADIX // halves_of))
                tail = TAIL if halves_of == 2 and shift and n == 0 else 0
                shape = (rows // halves_of + tail, 2 * local)
                outs.append(pltpu.VMEM(shape, jnp.float32))
                if shift == 0:
                    outs[-1] = jax.ShapeDtypeStruct(shape, jnp.float32)
    if final:
        outs += [pltpu.VMEM((components, cells // col_count, cells), jnp.float32)] * col_count
    else:
        outs += [pltpu.VMEM((cells, cells), jnp.float32)] * count
    out = pl.pallas_call(
        functools.partial(wave_kernel, first, count, final, plan),
        in_specs=[smem, hbm, hbm, hbm, hbm] + [vmem] * len(others),
        out_specs=[vmem] * len(outs),
        scratch_shapes=[
            pltpu.VMEM((count, 2, local, grid_len), jnp.float32),
            pltpu.VMEM(dft.shape, jnp.bfloat16),
            pltpu.VMEM(twiddle.shape, jnp.float32),
            pltpu.VMEM((2,) + mean.shape[2:], jnp.bfloat16),
            pltpu.VMEM((2 * local // LANES, quarter, LANES), jnp.float32),
            pltpu.VMEM((2, grid_len // LANES, local, LANES), jnp.float32),
            pltpu.SemaphoreType.DMA((count + 3,)),
        ],
        out_shape=outs,
        compiler_params=pltpu.CompilerParams(vmem_limit_bytes=16 << 20),
        name="transform_y",
    )(
        col,
        *[in_hbm(array) for array in (spectra, dft, twiddle, mean)],
        *[in_vmem(array) for array in others],
    )
    blocks = [[[] for _ in range(col_count)] for _ in range(count)]
    for array, (b, shift, _, _) in zip(out, plan):
        blocks[b][shift].append(array)
    return blocks, list(out[len(plan) :])


def field_kernel(component, first_row, col_count, col_ref, *refs):
    wave_refs, table_ref = refs[:col_count], refs[col_count]
    out_hbm, lane_ref, out_ref, sems = refs[-4:]
    rows, width = wave_refs[0].shape
    local = width // 2
    block = rows // RADIX
    col = col_ref[0]
    half_len = table_ref.shape[-1]
    chunk = 2 * LANES
    waves = []
    for parity in range(2):
        lanes = slice(parity * local, (parity + 1) * local)
        waves.append(split(jnp.concatenate([ref[:rows, lanes] for ref in wave_refs], axis=1)))
    sources = [lax.rem(col + col_count - shift, col_count) for shift in range(col_count)]
    copies = []
    for at in range(0, half_len, chunk):
        sums = []
        for parity in range(2):
            table = [
                jnp.concatenate(
                    [table_ref[half, source, parity, :, at : at + chunk] for source in sources],
                    axis=0,
                )
                for half in range(2)
            ]
            sums.append(product(waves[parity], table, NN))
        for side, field in enumerate((sums[0] + sums[1], sums[0] - sums[1])):
            start = side * half_len + at
            for lane in range(chunk // LANES):
                place = start // LANES + lane
                for t in range(RADIX):
                    lane_ref[place, pl.ds(t, block, stride=RADIX), :] = field[
                        t * block : (t + 1) * block, lane * LANES : (lane + 1) * LANES
                    ]
                out_ref[:, place * LANES : (place + 1) * LANES] = lane_ref[place]
            copy = pltpu.make_async_copy(
                out_ref.at[:, start : start + chunk],
                out_hbm.at[component, 0, first_row : first_row + rows, start : start + chunk],
                sems.at[len(copies)],
            )
            copy.start()
            copies.append(copy)
    for copy in copies:
        copy.wait()


def transform_x(col, waves, table, velocity, component, first_row, shape):
    rows, col_count = waves[0].shape[0], len(waves)
    in_specs = [pl.BlockSpec(memory_space=pltpu.SMEM)]
    in_specs += [pl.BlockSpec(memory_space=pltpu.VMEM)] * (col_count + 1)
    args = [col] + [in_vmem(array) for array in (*waves, table)]
    aliases = {}
    if velocity is not None:
        in_specs.append(pl.BlockSpec(memory_space=pl.ANY))
        aliases = {len(args): 0}
        args.append(velocity)
    return pl.pallas_call(
        functools.partial(field_kernel, component, first_row, col_count),
        in_specs=in_specs,
        out_specs=pl.BlockSpec(memory_space=pl.ANY),
        scratch_shapes=[
            pltpu.VMEM((shape[3] // LANES, rows, LANES), jnp.float32),
            pltpu.VMEM((rows, shape[3]), jnp.float32),
            pltpu.SemaphoreType.DMA((shape[3] // (2 * LANES),)),
        ],
        out_shape=jax.ShapeDtypeStruct(shape, jnp.float32),
        input_output_aliases=aliases,
        compiler_params=pltpu.CompilerParams(vmem_limit_bytes=16 << 20),
        name="transform_x",
    )(*args)


def project_kernel(count, steps_ref, *refs):
    part_refs, (history_ref, basis_ref, snap_ref, coeff_ref, sum_ref) = refs[:count], refs[count:]
    rank, height, cells = basis_ref.shape
    coarse = functools.reduce(jnp.add, [ref[...] for ref in part_refs])
    snap_ref[0] = coarse.reshape(height, cells).astype(jnp.bfloat16)
    for snap in range(1, SNAPS):
        snap_ref[snap] = history_ref[steps_ref[snap - 1]]

    def rows(ref, start, size):
        tiles = [
            ref[start : start + size, at : at + TILE, :].reshape(size * TILE, cells)
            for at in range(0, height, TILE)
        ]
        return jnp.concatenate(tiles, axis=1)

    right = rows(snap_ref, 0, SNAPS)
    group = 32
    shape = (group * TILE, SNAPS * TILE)
    same = lax.rem(lax.broadcasted_iota(jnp.int32, shape, 0), TILE) == lax.rem(
        lax.broadcasted_iota(jnp.int32, shape, 1), TILE
    )
    for start in range(0, rank, group):
        pairs = lax.dot_general(
            rows(basis_ref, start, group), right, NT, preferred_element_type=jnp.float32
        )
        wanted = jnp.where(same, pairs, 0.0).reshape(group, TILE, SNAPS * TILE)
        sum_ref[start : start + group, :] = jnp.sum(wanted, axis=1)
    shape = (SNAPS, SNAPS * TILE)
    fold = lax.broadcasted_iota(jnp.int32, shape, 1) // TILE == lax.broadcasted_iota(
        jnp.int32, shape, 0
    )
    coeff_ref[...] = lax.dot_general(
        jnp.where(fold, 1.0, 0.0), sum_ref[...], NT,
        precision=lax.Precision.HIGHEST, preferred_element_type=jnp.float32,
    )


def project(parts, history, steps, basis):
    vmem = pl.BlockSpec(memory_space=pltpu.VMEM)
    rank, cells = basis.shape[0], basis.shape[-1]
    basis, history = basis.reshape(rank, -1, cells), history.reshape(history.shape[0], -1, cells)
    height = basis.shape[1]
    return pl.pallas_call(
        functools.partial(project_kernel, len(parts)),
        in_specs=[pl.BlockSpec(memory_space=pltpu.SMEM)] + [vmem] * (len(parts) + 2),
        out_specs=[vmem, vmem],
        out_shape=[
            jax.ShapeDtypeStruct((SNAPS, height, cells), jnp.bfloat16),
            pltpu.VMEM((SNAPS, rank), jnp.float32),
        ],
        scratch_shapes=[pltpu.VMEM((rank, SNAPS * TILE), jnp.float32)],
        compiler_params=pltpu.CompilerParams(vmem_limit_bytes=16 << 20),
        name="project",
    )(steps, *[in_vmem(array) for array in (*parts, history, basis)])


def attach_kernel(sums_ref, *refs):
    for out_ref in refs[len(refs) // 2 :]:
        start = out_ref.shape[0] - TAIL
        for part in range(SNAPS // TAIL):
            out_ref[start:, part * LANES : part * LANES + SNAPS] = sums_ref[
                part * TAIL : (part + 1) * TAIL, :
            ]


def attach(sums, blocks):
    vmem = pl.BlockSpec(memory_space=pltpu.VMEM)
    return pl.pallas_call(
        attach_kernel,
        in_specs=[vmem] * (1 + len(blocks)),
        out_specs=[vmem] * len(blocks),
        out_shape=[pltpu.VMEM(block.shape, jnp.float32) for block in blocks],
        input_output_aliases={1 + n: n for n in range(len(blocks))},
        compiler_params=pltpu.CompilerParams(vmem_limit_bytes=16 << 20),
        name="attach",
    )(in_vmem(sums), *[in_vmem(block) for block in blocks])


def total_of(col, own_ref, block_refs, sum_ref):
    col_count = 1 + len(block_refs)
    sum_ref[col] = own_ref[...]
    for shift, block_ref in enumerate(block_refs, 1):
        source = lax.rem(col + col_count - shift, col_count)
        start = block_ref.shape[0] - TAIL
        for part in range(SNAPS // TAIL):
            sum_ref[source, part * TAIL : (part + 1) * TAIL, :] = block_ref[
                start:, part * LANES : part * LANES + SNAPS
            ]
    return functools.reduce(jnp.add, [sum_ref[source] for source in range(col_count)])


def finish_kernel(total_rows, col_count, col_ref, gram_ref, *refs):
    block_refs = refs[: col_count - 1]
    residual_ref, factor_ref, ortho_ref, sum_ref = refs[col_count - 1 :]
    gram = total_of(col_ref[0], gram_ref, block_refs, sum_ref)
    size = gram_ref.shape[0]
    row = lax.broadcasted_iota(jnp.int32, (size, size), 0)
    column = lax.broadcasted_iota(jnp.int32, (size, size), 1)
    upper = gram / total_rows
    inverse = jnp.where(row == column, 1.0, 0.0)
    for step in range(size):
        upper_row, inverse_row = upper[step : step + 1, :], inverse[step : step + 1, :]
        below = jnp.sum(jnp.where(column == step, upper, 0.0), axis=1, keepdims=True)
        pivot = below[step : step + 1, :]
        scale = 1.0 / jnp.sqrt(pivot)
        ratio = jnp.where(row > step, below / pivot, 0.0)
        upper = jnp.where(row == step, upper_row * scale, upper - ratio * upper_row)
        inverse = jnp.where(row == step, inverse_row * scale, inverse - ratio * inverse_row)
    factor_ref[...] = jnp.where(column >= row, upper, 0.0)
    ortho = jnp.dot(
        inverse, residual_ref[...], precision=lax.Precision.HIGHEST,
        preferred_element_type=jnp.float32,
    )
    cells = ortho_ref.shape[-1]
    for at in range(ortho_ref.shape[1]):
        ortho_ref[:, at, :] = ortho[:, at * cells : (at + 1) * cells]


def finish(col, gram, blocks, residual, cells, total_rows):
    vmem = pl.BlockSpec(memory_space=pltpu.VMEM)
    size, col_count = gram.shape[0], 1 + len(blocks)
    return pl.pallas_call(
        functools.partial(finish_kernel, total_rows, col_count),
        in_specs=[pl.BlockSpec(memory_space=pltpu.SMEM)] + [vmem] * (col_count + 1),
        out_specs=[vmem, vmem],
        out_shape=[
            jax.ShapeDtypeStruct((size, size), jnp.float32),
            jax.ShapeDtypeStruct((size, residual.shape[1] // cells, cells), jnp.float32),
        ],
        scratch_shapes=[pltpu.VMEM((col_count, size, size), jnp.float32)],
        compiler_params=pltpu.CompilerParams(vmem_limit_bytes=16 << 20),
        name="finish",
    )(col, gram, *[in_vmem(block) for block in blocks], residual)


def swap(value, axis, bit):
    size = lax.axis_size(axis)
    return lax.ppermute(value, axis, [(i, i ^ bit) for i in range(size)])


def sum_over(value, axis):
    bit, size = 1, lax.axis_size(axis)
    while bit < size:
        bits = (size // bit).bit_length() - 1
        if bits % 2 == 0:
            one, two, three = (swap(value, axis, bit * n) for n in (1, 2, 3))
            value = (value + one) + (two + three)
            bit *= 4
        else:
            value = value + swap(value, axis, bit)
            bit *= 2
    return value


def split_coeffs(coeffs):
    coeffs_high = coeffs.astype(jnp.bfloat16)
    high_wide = lax.optimization_barrier(coeffs_high).astype(jnp.float32)
    coeffs_low = (coeffs - high_wide).astype(jnp.bfloat16)
    return coeffs_high, lax.optimization_barrier(coeffs_low)


def residual_of(parts, snap_flat, basis):
    projected = jnp.dot(
        parts, basis.reshape(basis.shape[0], -1), preferred_element_type=jnp.float32
    )
    residual = snap_flat.astype(jnp.float32) - (projected[:SNAPS] + projected[SNAPS:])
    return residual, lax.dot_general(residual, residual, NT, precision=lax.Precision.HIGHEST)


def rows_of(residual):
    return residual.shape[1] * lax.axis_size("row") * lax.axis_size("col")


def body(spectra, history, steps, basis):
    grid_len = spectra.shape[4]
    components = spectra.shape[1]
    col_count = lax.axis_size("col")
    mode_count = spectra.shape[3] * col_count
    consts = [jnp.asarray(table) for table in tables(grid_len, mode_count, col_count, STRIDE)]
    col = lax.axis_index("col").astype(jnp.int32).reshape(1)
    groups = [(0, 1), (1, components - 1)]
    waves, parts, last = [], [], components - 1
    for first, count in groups:
        final = first + count == components
        blocks, parts = transform_y(col, spectra, consts, parts, first, count, col_count, final)
        waves += blocks

    def send(block, shift):
        perm = [(i, (i + shift) % col_count) for i in range(col_count)]
        return lax.ppermute(block, "col", perm)

    shifts = range(1, col_count)
    for shift in shifts:
        parts[shift] = send(parts[shift], shift)
        for component in range(last):
            block = waves[component][shift][0]
            waves[component][shift] = [send(block, shift)]
    snapshots, coeffs = project(parts, history, steps, basis)
    coeffs = sum_over(sum_over(coeffs, "col"), "row")
    coeff_parts = jnp.concatenate(split_coeffs(coeffs), axis=0)
    residual, gram = residual_of(coeff_parts, snapshots.reshape(SNAPS, -1), basis)
    gram = sum_over(gram, "row")
    heads = attach(gram, [waves[last][shift][0] for shift in shifts])
    for shift in shifts:
        head = send(heads[shift - 1], shift)
        waves[last][shift] = [head, send(waves[last][shift][1], shift)]
    shape = (components, 1, grid_len // col_count, grid_len)
    velocity = None

    def fill(component, velocity):
        row = 0
        for arrays in zip(*waves[component]):
            velocity = transform_x(col, arrays, consts[2], velocity, component, row, shape)
            row += arrays[0].shape[0]
        return velocity

    for component in range(last):
        velocity = fill(component, velocity)
    velocity, own_gram = lax.optimization_barrier((velocity, gram))
    factor, ortho = finish(
        col, own_gram, [waves[last][shift][0] for shift in shifts], residual, history.shape[-1],
        rows_of(residual),
    )
    for component in range(last, components):
        velocity = fill(component, velocity)
    return velocity, coeffs.T, factor, ortho.reshape(history.shape)


def body_general(spectra, history, steps, basis):
    highest = lax.Precision.HIGHEST
    grid_len = spectra.shape[4]
    col_count = lax.axis_size("col")
    mode_count = spectra.shape[3] * col_count
    index_y = jnp.arange(grid_len, dtype=jnp.int32)
    phase_y = (
        2.0
        * math.pi
        / grid_len
        * (index_y[:, None] * index_y[None, :] % grid_len).astype(jnp.float32)
    )
    cos_y = jnp.cos(phase_y)
    sin_y = jnp.sin(phase_y)
    wave_real = jnp.dot(spectra[0], cos_y, precision=highest) - jnp.dot(
        spectra[1], sin_y, precision=highest
    )
    wave_imag = jnp.dot(spectra[0], sin_y, precision=highest) + jnp.dot(
        spectra[1], cos_y, precision=highest
    )
    wave = jnp.stack([wave_real, wave_imag])
    modes_x = jnp.arange(mode_count, dtype=jnp.int32)
    phase_x = (
        2.0
        * math.pi
        / grid_len
        * (modes_x[:, None] * index_y[None, :] % grid_len).astype(jnp.float32)
    )
    weight_x = jnp.where(modes_x == 0, 1.0, 2.0).astype(jnp.float32)[:, None] / grid_len
    table_x = jnp.stack([weight_x * jnp.cos(phase_x), -weight_x * jnp.sin(phase_x)])
    velocity = lax.dot_general(
        lax.all_to_all(wave, "col", split_axis=4, concat_axis=3, tiled=True),
        table_x,
        (((0, 3), (0, 1)), ((), ())),
        precision=highest,
    )
    components, planes, local_y, _ = velocity.shape
    coarse = (
        velocity.reshape(components, planes, local_y // STRIDE, STRIDE, grid_len // STRIDE, STRIDE)
        .mean(axis=(3, 5))
        .astype(jnp.bfloat16)
    )
    chosen = jnp.take(history, steps[: SNAPS - 1], axis=0)
    snap_flat = jnp.concatenate([coarse[None], chosen], axis=0).reshape(SNAPS, -1)
    basis_flat = basis.reshape(basis.shape[0], -1)
    coeffs = lax.dot_general(snap_flat, basis_flat, NT, preferred_element_type=jnp.float32)
    coeffs = sum_over(sum_over(coeffs, "col"), "row")
    parts = jnp.concatenate(split_coeffs(coeffs), axis=0)
    residual, gram = residual_of(parts, snap_flat, basis)
    gram = sum_over(sum_over(gram, "col"), "row") / rows_of(residual)
    lower_factor = jnp.linalg.cholesky(gram)
    ortho = lax.linalg.triangular_solve(lower_factor, residual, left_side=True, lower=True)
    return velocity, coeffs.T, lower_factor.T, ortho.reshape((SNAPS,) + coarse.shape)


def solution(mesh):
    in_specs = (
        P(None, None, "row", "col", None),
        P(None, None, "row", "col", None),
        P(),
        P(None, None, "row", "col", None),
    )
    out_specs = (P(None, "row", "col", None), P(), P(), P(None, None, "row", "col", None))

    rows, cols = mesh.shape["row"], mesh.shape["col"]

    def mapped(local_body):
        return jax.shard_map(
            local_body, mesh=mesh, in_specs=in_specs, out_specs=out_specs, check_vma=False
        )

    def step(spectra, history, steps, basis):
        local = spectra.shape[3] // cols
        height = spectra.shape[1] * history.shape[3] // cols
        apart = spectra.shape[2] != rows or spectra.shape[1] < 3 or cols < 4
        if apart or local % LANES or height % TILE:
            return mapped(body_general)(spectra, history, steps, basis)

        return mapped(body)(spectra, history, steps, basis)

    return step
```

```python
import functools
import math

import jax
import jax.numpy as jnp
import ml_dtypes
import numpy as np
from jax import lax
from jax.experimental import pallas as pl
from jax.experimental.pallas import tpu as pltpu
from jax.sharding import PartitionSpec as P


STRIDE = 8
SNAPS = 16
RADIX = 4
LANES = 128
TAIL = 8
TILE = 16
NT = (((1,), (1,)), ((), ()))
NN = (((1,), (0,)), ((), ()))


def halves(table):
    table = table.astype(np.float32)
    high = table.astype(ml_dtypes.bfloat16)
    low = (table - high.astype(np.float32)).astype(ml_dtypes.bfloat16)
    return np.stack([high, low])


@functools.lru_cache(maxsize=None)
def tables(grid_len, mode_count, col_count, stride):
    local = mode_count // col_count
    quarter = grid_len // RADIX
    index = np.arange(quarter)
    phase = 2.0 * np.pi / quarter * (index[:, None] * index[None, :] % quarter)
    dft = halves(np.concatenate([np.cos(phase), -np.sin(phase)], axis=1))
    twiddle_phase = 2.0 * np.pi / grid_len * np.arange(RADIX)[:, None] * index[None, :]
    twiddle = np.zeros((2 * RADIX, quarter), np.float32)
    twiddle[0::2] = np.cos(twiddle_phase)
    twiddle[1::2] = np.sin(twiddle_phase)
    modes = np.arange(mode_count)
    weight = np.where(modes == 0, 1.0, 2.0)[:, None] / grid_len
    place = np.arange(grid_len)
    phase = 2.0 * np.pi / grid_len * (modes[:, None] * place[None, :] % grid_len)
    full = np.stack([weight * np.cos(phase), -weight * np.sin(phase)])
    full = full.reshape(2, col_count, local // 2, 2, grid_len).transpose(1, 3, 0, 2, 4)
    along_x = halves(full.reshape(col_count, 2, local, grid_len)[..., : grid_len // 2])
    mean = full.reshape(col_count, 2 * local, grid_len // stride, stride).sum(-1) / stride**2
    return dft, twiddle, along_x, halves(mean)


def in_hbm(array):
    return pltpu.with_memory_space_constraint(array, pltpu.HBM)


def in_vmem(array):
    return pltpu.with_memory_space_constraint(array, pltpu.VMEM)


def split(value):
    high = value.astype(jnp.bfloat16)
    return high, (value - high.astype(jnp.float32)).astype(jnp.bfloat16)


def product(left, right, dims):
    dot = functools.partial(
        lax.dot_general, dimension_numbers=dims, preferred_element_type=jnp.float32
    )
    return dot(left[0], right[0]) + (dot(left[0], right[1]) + dot(left[1], right[0]))


def wave_kernel(first, count, final, plan, col_ref, spec_hbm, dft_hbm, twiddle_hbm, mean_hbm, *refs):
    dft_ref, twiddle_ref, mean_ref, sum_ref, lane_ref, sems = refs[-6:]
    others, refs = refs[: first if final else 0], refs[first if final else 0 : -6]
    local, grid_len = spec_hbm.shape[-2:]
    lanes = grid_len // LANES
    quarter = grid_len // RADIX
    col_count = 1 + max(shift for _, shift, _, _ in plan)
    out_refs, part_refs = refs[: len(plan)], refs[len(plan) :]
    block = quarter // col_count
    col = col_ref[0]
    arrivals = [
        [
            pltpu.make_async_copy(
                spec_hbm.at[:, first + b, 0, :, lane * LANES : (lane + 1) * LANES],
                lane_ref.at[b, :, lane],
                sems.at[b * lanes + lane],
            )
            for lane in range(lanes)
        ]
        for b in range(count)
    ]
    ready = [
        pltpu.make_async_copy(dft_hbm, dft_ref, sems.at[count * lanes]),
        pltpu.make_async_copy(twiddle_hbm, twiddle_ref, sems.at[count * lanes + 1]),
    ]
    mean_copy = pltpu.make_async_copy(mean_hbm.at[:, col], mean_ref, sems.at[count * lanes + 2])
    for copy in (*arrivals[0], *ready, mean_copy, *sum(arrivals[1:], [])):
        copy.start()
    starts = [
        pl.multiple_of(lax.rem(col + shift, col_count) * block, block) for shift in range(col_count)
    ]
    for b in range(count):
        for copy in arrivals[b] + (ready if b == 0 else []):
            copy.wait()
        dft = [
            jnp.concatenate([dft_ref[half, pl.ds(start, block), :] for start in starts], axis=0)
            for half in range(2)
        ]

        def piece(parity, part, r):
            per = quarter // LANES
            rows = pl.ds(parity, local // 2, stride=2)
            return jnp.concatenate(
                [lane_ref[b, part, lane, rows, :] for lane in range(r * per, (r + 1) * per)], axis=1
            )

        even_odd = {}
        for parity in range(2):
            for part in range(2):
                s0, s1, s2, s3 = [piece(parity, part, r) for r in range(RADIX)]
                even_odd[parity, part] = (s0 + s2, s1 + s3, s0 - s2, s1 - s3)
        for t in range(RADIX):
            cosine, sine = twiddle_ref[2 * t : 2 * t + 1, :], twiddle_ref[2 * t + 1 : 2 * t + 2, :]
            first_half, second_half = [[], []], [[], []]
            for parity in range(2):
                re, im = even_odd[parity, 0], even_odd[parity, 1]
                if t == 0:
                    u_re, u_im = re[0] + re[1], im[0] + im[1]
                elif t == 2:
                    u_re, u_im = re[0] - re[1], im[0] - im[1]
                elif t == 1:
                    u_re, u_im = re[2] - im[3], im[2] + re[3]
                else:
                    u_re, u_im = re[2] + im[3], im[2] - re[3]
                if t == 0:
                    v_re, v_im = u_re, u_im
                else:
                    v_re = u_re * cosine - u_im * sine
                    v_im = u_re * sine + u_im * cosine
                high_re, low_re = split(v_re)
                high_im, low_im = split(v_im)
                for side, (part_re, part_im) in enumerate(((high_re, high_im), (low_re, low_im))):
                    first_half[side] += [part_re, part_im]
                    second_half[side] += [part_im, -part_re]
            rows = [
                jnp.concatenate(
                    [jnp.concatenate(one, axis=0), jnp.concatenate(two, axis=0)], axis=1
                )
                for one, two in zip(first_half, second_half)
            ]
            wave = product(dft, rows, NT)
            for out_ref, (at, shift, n, size) in zip(out_refs, plan):
                if at == b:
                    start = shift * block + n * size
                    out_ref[t * size : (t + 1) * size, :] = wave[start : start + size]
            for lane in range(2 * local // LANES):
                some = wave[:, lane * LANES : (lane + 1) * LANES]
                sum_ref[lane] = some if t == 0 else sum_ref[lane] + some
        if b == 0:
            mean_copy.wait()
        pair = STRIDE // RADIX
        total = []
        for lane in range(2 * local // LANES):
            steps = [sum_ref[lane, pl.ds(n, quarter // pair, stride=pair), :] for n in range(pair)]
            total.append(functools.reduce(jnp.add, steps))
        total = jnp.concatenate(total, axis=1)
        mean = product(split(total), (mean_ref[0], mean_ref[1]), NN)
        if final:
            per = mean.shape[0] // col_count
            for shift in range(col_count):
                part_refs[shift][first + b] = mean[shift * per : (shift + 1) * per]
        else:
            part_refs[b][...] = mean
    for at, other in enumerate(others):
        per = other.shape[0] // col_count
        for shift in range(col_count):
            part_refs[shift][at] = other[shift * per : (shift + 1) * per]


def transform_y(col, spectra, consts, others, first, count, col_count, final):
    dft, twiddle, _, mean = consts
    components, (local, grid_len) = spectra.shape[1], spectra.shape[-2:]
    quarter = grid_len // RADIX
    rows = grid_len // col_count
    cells = grid_len // STRIDE
    vmem, hbm = pl.BlockSpec(memory_space=pltpu.VMEM), pl.BlockSpec(memory_space=pltpu.HBM)
    smem = pl.BlockSpec(memory_space=pltpu.SMEM)
    plan, outs = [], []
    for b in range(count):
        for shift in range(col_count):
            halves_of = 2 if final and b == count - 1 else 1
            for n in range(halves_of):
                plan.append((b, shift, n, rows // RADIX // halves_of))
                tail = TAIL if halves_of == 2 and shift and n == 0 else 0
                shape = (rows // halves_of + tail, 2 * local)
                outs.append(pltpu.VMEM(shape, jnp.float32))
                if shift == 0:
                    outs[-1] = jax.ShapeDtypeStruct(shape, jnp.float32)
    if final:
        outs += [pltpu.VMEM((components, cells // col_count, cells), jnp.float32)] * col_count
    else:
        outs += [pltpu.VMEM((cells, cells), jnp.float32)] * count
    out = pl.pallas_call(
        functools.partial(wave_kernel, first, count, final, plan),
        in_specs=[smem, hbm, hbm, hbm, hbm] + [vmem] * len(others),
        out_specs=[vmem] * len(outs),
        scratch_shapes=[
            pltpu.VMEM(dft.shape, jnp.bfloat16),
            pltpu.VMEM(twiddle.shape, jnp.float32),
            pltpu.VMEM((2,) + mean.shape[2:], jnp.bfloat16),
            pltpu.VMEM((2 * local // LANES, quarter, LANES), jnp.float32),
            pltpu.VMEM((count, 2, grid_len // LANES, local, LANES), jnp.float32),
            pltpu.SemaphoreType.DMA((count * (grid_len // LANES) + 3,)),
        ],
        out_shape=outs,
        compiler_params=pltpu.CompilerParams(vmem_limit_bytes=16 << 20),
        name="transform_y",
    )(
        col,
        *[in_hbm(array) for array in (spectra, dft, twiddle, mean)],
        *[in_vmem(array) for array in others],
    )
    blocks = [[[] for _ in range(col_count)] for _ in range(count)]
    for array, (b, shift, _, _) in zip(out, plan):
        blocks[b][shift].append(array)
    return blocks, list(out[len(plan) :])


def field_kernel(component, first_row, col_count, col_ref, *refs):
    wave_refs, table_ref = refs[:col_count], refs[col_count]
    out_hbm, lane_ref, out_ref, sems = refs[-4:]
    rows, width = wave_refs[0].shape
    local = width // 2
    block = rows // RADIX
    col = col_ref[0]
    half_len = table_ref.shape[-1]
    chunk = 2 * LANES
    waves = []
    for parity in range(2):
        lanes = slice(parity * local, (parity + 1) * local)
        waves.append(split(jnp.concatenate([ref[:rows, lanes] for ref in wave_refs], axis=1)))
    sources = [lax.rem(col + col_count - shift, col_count) for shift in range(col_count)]
    copies = []
    for at in range(0, half_len, chunk):
        sums = []
        for parity in range(2):
            table = [
                jnp.concatenate(
                    [table_ref[half, source, parity, :, at : at + chunk] for source in sources],
                    axis=0,
                )
                for half in range(2)
            ]
            sums.append(product(waves[parity], table, NN))
        for side, field in enumerate((sums[0] + sums[1], sums[0] - sums[1])):
            start = side * half_len + at
            for lane in range(chunk // LANES):
                place = start // LANES + lane
                for t in range(RADIX):
                    lane_ref[place, pl.ds(t, block, stride=RADIX), :] = field[
                        t * block : (t + 1) * block, lane * LANES : (lane + 1) * LANES
                    ]
                out_ref[:, place * LANES : (place + 1) * LANES] = lane_ref[place]
            copy = pltpu.make_async_copy(
                out_ref.at[:, start : start + chunk],
                out_hbm.at[component, 0, first_row : first_row + rows, start : start + chunk],
                sems.at[len(copies)],
            )
            copy.start()
            copies.append(copy)
    for copy in copies:
        copy.wait()


def transform_x(col, waves, table, velocity, component, first_row, shape):
    rows, col_count = waves[0].shape[0], len(waves)
    in_specs = [pl.BlockSpec(memory_space=pltpu.SMEM)]
    in_specs += [pl.BlockSpec(memory_space=pltpu.VMEM)] * (col_count + 1)
    args = [col] + [in_vmem(array) for array in (*waves, table)]
    aliases = {}
    if velocity is not None:
        in_specs.append(pl.BlockSpec(memory_space=pl.ANY))
        aliases = {len(args): 0}
        args.append(velocity)
    return pl.pallas_call(
        functools.partial(field_kernel, component, first_row, col_count),
        in_specs=in_specs,
        out_specs=pl.BlockSpec(memory_space=pl.ANY),
        scratch_shapes=[
            pltpu.VMEM((shape[3] // LANES, rows, LANES), jnp.float32),
            pltpu.VMEM((rows, shape[3]), jnp.float32),
            pltpu.SemaphoreType.DMA((shape[3] // (2 * LANES),)),
        ],
        out_shape=jax.ShapeDtypeStruct(shape, jnp.float32),
        input_output_aliases=aliases,
        compiler_params=pltpu.CompilerParams(vmem_limit_bytes=16 << 20),
        name="transform_x",
    )(*args)


def project_kernel(count, steps_ref, *refs):
    part_refs, (history_ref, basis_ref, snap_ref, coeff_ref, sum_ref) = refs[:count], refs[count:]
    rank, height, cells = basis_ref.shape
    coarse = functools.reduce(jnp.add, [ref[...] for ref in part_refs])
    snap_ref[0] = coarse.reshape(height, cells).astype(jnp.bfloat16)
    for snap in range(1, SNAPS):
        snap_ref[snap] = history_ref[steps_ref[snap - 1]]

    def rows(ref, start, size):
        tiles = [
            ref[start : start + size, at : at + TILE, :].reshape(size * TILE, cells)
            for at in range(0, height, TILE)
        ]
        return jnp.concatenate(tiles, axis=1)

    right = rows(snap_ref, 0, SNAPS)
    group = 32
    shape = (group * TILE, SNAPS * TILE)
    same = lax.rem(lax.broadcasted_iota(jnp.int32, shape, 0), TILE) == lax.rem(
        lax.broadcasted_iota(jnp.int32, shape, 1), TILE
    )
    for start in range(0, rank, group):
        pairs = lax.dot_general(
            rows(basis_ref, start, group), right, NT, preferred_element_type=jnp.float32
        )
        wanted = jnp.where(same, pairs, 0.0).reshape(group, TILE, SNAPS * TILE)
        sum_ref[start : start + group, :] = jnp.sum(wanted, axis=1)
    shape = (SNAPS, SNAPS * TILE)
    fold = lax.broadcasted_iota(jnp.int32, shape, 1) // TILE == lax.broadcasted_iota(
        jnp.int32, shape, 0
    )
    coeff_ref[...] = lax.dot_general(
        jnp.where(fold, 1.0, 0.0), sum_ref[...], NT,
        precision=lax.Precision.HIGHEST, preferred_element_type=jnp.float32,
    )


def project(parts, history, steps, basis):
    vmem = pl.BlockSpec(memory_space=pltpu.VMEM)
    rank, cells = basis.shape[0], basis.shape[-1]
    basis, history = basis.reshape(rank, -1, cells), history.reshape(history.shape[0], -1, cells)
    height = basis.shape[1]
    return pl.pallas_call(
        functools.partial(project_kernel, len(parts)),
        in_specs=[pl.BlockSpec(memory_space=pltpu.SMEM)] + [vmem] * (len(parts) + 2),
        out_specs=[vmem, vmem],
        out_shape=[
            jax.ShapeDtypeStruct((SNAPS, height, cells), jnp.bfloat16),
            pltpu.VMEM((SNAPS, rank), jnp.float32),
        ],
        scratch_shapes=[pltpu.VMEM((rank, SNAPS * TILE), jnp.float32)],
        compiler_params=pltpu.CompilerParams(vmem_limit_bytes=16 << 20),
        name="project",
    )(steps, *[in_vmem(array) for array in (*parts, history, basis)])


def attach_kernel(sums_ref, *refs):
    for out_ref in refs[len(refs) // 2 :]:
        start = out_ref.shape[0] - TAIL
        for part in range(SNAPS // TAIL):
            out_ref[start:, part * LANES : part * LANES + SNAPS] = sums_ref[
                part * TAIL : (part + 1) * TAIL, :
            ]


def attach(sums, blocks):
    vmem = pl.BlockSpec(memory_space=pltpu.VMEM)
    return pl.pallas_call(
        attach_kernel,
        in_specs=[vmem] * (1 + len(blocks)),
        out_specs=[vmem] * len(blocks),
        out_shape=[pltpu.VMEM(block.shape, jnp.float32) for block in blocks],
        input_output_aliases={1 + n: n for n in range(len(blocks))},
        compiler_params=pltpu.CompilerParams(vmem_limit_bytes=16 << 20),
        name="attach",
    )(in_vmem(sums), *[in_vmem(block) for block in blocks])


def total_of(col, own_ref, block_refs, sum_ref):
    col_count = 1 + len(block_refs)
    sum_ref[col] = own_ref[...]
    for shift, block_ref in enumerate(block_refs, 1):
        source = lax.rem(col + col_count - shift, col_count)
        start = block_ref.shape[0] - TAIL
        for part in range(SNAPS // TAIL):
            sum_ref[source, part * TAIL : (part + 1) * TAIL, :] = block_ref[
                start:, part * LANES : part * LANES + SNAPS
            ]
    return functools.reduce(jnp.add, [sum_ref[source] for source in range(col_count)])


def finish_kernel(total_rows, col_count, col_ref, gram_ref, *refs):
    block_refs = refs[: col_count - 1]
    residual_ref, factor_ref, ortho_ref, sum_ref = refs[col_count - 1 :]
    gram = total_of(col_ref[0], gram_ref, block_refs, sum_ref)
    size = gram_ref.shape[0]
    row = lax.broadcasted_iota(jnp.int32, (size, size), 0)
    column = lax.broadcasted_iota(jnp.int32, (size, size), 1)
    upper = gram / total_rows
    inverse = jnp.where(row == column, 1.0, 0.0)
    for step in range(size):
        upper_row, inverse_row = upper[step : step + 1, :], inverse[step : step + 1, :]
        below = jnp.sum(jnp.where(column == step, upper, 0.0), axis=1, keepdims=True)
        pivot = below[step : step + 1, :]
        scale = 1.0 / jnp.sqrt(pivot)
        ratio = jnp.where(row > step, below / pivot, 0.0)
        upper = jnp.where(row == step, upper_row * scale, upper - ratio * upper_row)
        inverse = jnp.where(row == step, inverse_row * scale, inverse - ratio * inverse_row)
    factor_ref[...] = jnp.where(column >= row, upper, 0.0)
    ortho = jnp.dot(
        inverse, residual_ref[...], precision=lax.Precision.HIGHEST,
        preferred_element_type=jnp.float32,
    )
    cells = ortho_ref.shape[-1]
    for at in range(ortho_ref.shape[1]):
        ortho_ref[:, at, :] = ortho[:, at * cells : (at + 1) * cells]


def finish(col, gram, blocks, residual, cells, total_rows):
    vmem = pl.BlockSpec(memory_space=pltpu.VMEM)
    size, col_count = gram.shape[0], 1 + len(blocks)
    return pl.pallas_call(
        functools.partial(finish_kernel, total_rows, col_count),
        in_specs=[pl.BlockSpec(memory_space=pltpu.SMEM)] + [vmem] * (col_count + 1),
        out_specs=[vmem, vmem],
        out_shape=[
            jax.ShapeDtypeStruct((size, size), jnp.float32),
            jax.ShapeDtypeStruct((size, residual.shape[1] // cells, cells), jnp.float32),
        ],
        scratch_shapes=[pltpu.VMEM((col_count, size, size), jnp.float32)],
        compiler_params=pltpu.CompilerParams(vmem_limit_bytes=16 << 20),
        name="finish",
    )(col, gram, *[in_vmem(block) for block in blocks], residual)


def swap(value, axis, bit):
    size = lax.axis_size(axis)
    return lax.ppermute(value, axis, [(i, i ^ bit) for i in range(size)])


def sum_over(value, axis):
    bit, size = 1, lax.axis_size(axis)
    while bit < size:
        bits = (size // bit).bit_length() - 1
        if bits % 2 == 0:
            one, two, three = (swap(value, axis, bit * n) for n in (1, 2, 3))
            value = (value + one) + (two + three)
            bit *= 4
        else:
            value = value + swap(value, axis, bit)
            bit *= 2
    return value


def split_coeffs(coeffs):
    coeffs_high = coeffs.astype(jnp.bfloat16)
    high_wide = lax.optimization_barrier(coeffs_high).astype(jnp.float32)
    coeffs_low = (coeffs - high_wide).astype(jnp.bfloat16)
    return coeffs_high, lax.optimization_barrier(coeffs_low)


def residual_of(parts, snap_flat, basis):
    projected = jnp.dot(
        parts, basis.reshape(basis.shape[0], -1), preferred_element_type=jnp.float32
    )
    residual = snap_flat.astype(jnp.float32) - (projected[:SNAPS] + projected[SNAPS:])
    return residual, lax.dot_general(residual, residual, NT, precision=lax.Precision.HIGHEST)


def rows_of(residual):
    return residual.shape[1] * lax.axis_size("row") * lax.axis_size("col")


def body(spectra, history, steps, basis):
    grid_len = spectra.shape[4]
    components = spectra.shape[1]
    col_count = lax.axis_size("col")
    mode_count = spectra.shape[3] * col_count
    consts = [jnp.asarray(table) for table in tables(grid_len, mode_count, col_count, STRIDE)]
    col = lax.axis_index("col").astype(jnp.int32).reshape(1)
    groups = [(0, 1), (1, components - 1)]
    waves, parts, last = [], [], components - 1
    for first, count in groups:
        final = first + count == components
        blocks, parts = transform_y(col, spectra, consts, parts, first, count, col_count, final)
        waves += blocks

    def send(block, shift):
        perm = [(i, (i + shift) % col_count) for i in range(col_count)]
        return lax.ppermute(block, "col", perm)

    shifts = range(1, col_count)
    for shift in shifts:
        parts[shift] = send(parts[shift], shift)
        for component in range(last):
            block = waves[component][shift][0]
            waves[component][shift] = [send(block, shift)]
    snapshots, coeffs = project(parts, history, steps, basis)
    coeffs = sum_over(sum_over(coeffs, "col"), "row")
    coeff_parts = jnp.concatenate(split_coeffs(coeffs), axis=0)
    residual, gram = residual_of(coeff_parts, snapshots.reshape(SNAPS, -1), basis)
    gram = sum_over(gram, "row")
    heads = attach(gram, [waves[last][shift][0] for shift in shifts])
    for shift in shifts:
        head = send(heads[shift - 1], shift)
        waves[last][shift] = [head, send(waves[last][shift][1], shift)]
    shape = (components, 1, grid_len // col_count, grid_len)
    velocity = None

    def fill(component, velocity):
        row = 0
        for arrays in zip(*waves[component]):
            velocity = transform_x(col, arrays, consts[2], velocity, component, row, shape)
            row += arrays[0].shape[0]
        return velocity

    for component in range(last):
        velocity = fill(component, velocity)
    velocity, own_gram = lax.optimization_barrier((velocity, gram))
    factor, ortho = finish(
        col, own_gram, [waves[last][shift][0] for shift in shifts], residual, history.shape[-1],
        rows_of(residual),
    )
    for component in range(last, components):
        velocity = fill(component, velocity)
    return velocity, coeffs.T, factor, ortho.reshape(history.shape)


def body_general(spectra, history, steps, basis):
    highest = lax.Precision.HIGHEST
    grid_len = spectra.shape[4]
    col_count = lax.axis_size("col")
    mode_count = spectra.shape[3] * col_count
    index_y = jnp.arange(grid_len, dtype=jnp.int32)
    phase_y = (
        2.0
        * math.pi
        / grid_len
        * (index_y[:, None] * index_y[None, :] % grid_len).astype(jnp.float32)
    )
    cos_y = jnp.cos(phase_y)
    sin_y = jnp.sin(phase_y)
    wave_real = jnp.dot(spectra[0], cos_y, precision=highest) - jnp.dot(
        spectra[1], sin_y, precision=highest
    )
    wave_imag = jnp.dot(spectra[0], sin_y, precision=highest) + jnp.dot(
        spectra[1], cos_y, precision=highest
    )
    wave = jnp.stack([wave_real, wave_imag])
    modes_x = jnp.arange(mode_count, dtype=jnp.int32)
    phase_x = (
        2.0
        * math.pi
        / grid_len
        * (modes_x[:, None] * index_y[None, :] % grid_len).astype(jnp.float32)
    )
    weight_x = jnp.where(modes_x == 0, 1.0, 2.0).astype(jnp.float32)[:, None] / grid_len
    table_x = jnp.stack([weight_x * jnp.cos(phase_x), -weight_x * jnp.sin(phase_x)])
    velocity = lax.dot_general(
        lax.all_to_all(wave, "col", split_axis=4, concat_axis=3, tiled=True),
        table_x,
        (((0, 3), (0, 1)), ((), ())),
        precision=highest,
    )
    components, planes, local_y, _ = velocity.shape
    coarse = (
        velocity.reshape(components, planes, local_y // STRIDE, STRIDE, grid_len // STRIDE, STRIDE)
        .mean(axis=(3, 5))
        .astype(jnp.bfloat16)
    )
    chosen = jnp.take(history, steps[: SNAPS - 1], axis=0)
    snap_flat = jnp.concatenate([coarse[None], chosen], axis=0).reshape(SNAPS, -1)
    basis_flat = basis.reshape(basis.shape[0], -1)
    coeffs = lax.dot_general(snap_flat, basis_flat, NT, preferred_element_type=jnp.float32)
    coeffs = sum_over(sum_over(coeffs, "col"), "row")
    parts = jnp.concatenate(split_coeffs(coeffs), axis=0)
    residual, gram = residual_of(parts, snap_flat, basis)
    gram = sum_over(sum_over(gram, "col"), "row") / rows_of(residual)
    lower_factor = jnp.linalg.cholesky(gram)
    ortho = lax.linalg.triangular_solve(lower_factor, residual, left_side=True, lower=True)
    return velocity, coeffs.T, lower_factor.T, ortho.reshape((SNAPS,) + coarse.shape)


def solution(mesh):
    in_specs = (
        P(None, None, "row", "col", None),
        P(None, None, "row", "col", None),
        P(),
        P(None, None, "row", "col", None),
    )
    out_specs = (P(None, "row", "col", None), P(), P(), P(None, None, "row", "col", None))

    rows, cols = mesh.shape["row"], mesh.shape["col"]

    def mapped(local_body):
        return jax.shard_map(
            local_body, mesh=mesh, in_specs=in_specs, out_specs=out_specs, check_vma=False
        )

    def step(spectra, history, steps, basis):
        local = spectra.shape[3] // cols
        height = spectra.shape[1] * history.shape[3] // cols
        apart = spectra.shape[2] != rows or spectra.shape[1] < 3 or cols < 4
        if apart or local % LANES or height % TILE:
            return mapped(body_general)(spectra, history, steps, basis)

        return mapped(body)(spectra, history, steps, basis)

    return step
```
